32 devices in a mesh: tensor: 2 (over y), dp: 16 (over z, x, core).
Axes of the slice: x: 2, y: 2, z: 4, core: 2. Of those that a mesh axis runs over, the one named last changes fastest.
Arguments:
- inputs: bfloat16 [2, 4096, 768], P(None, 'dp'), may hold values from -6 to 6
- cotangent: bfloat16 [2, 4096, 768], P(None, 'dp'), may hold values from -6 to 6
- segments: int32 [2, 4096], replicated, may hold values from 0 to 31, never falling along the last dimension, each value on 1 to 512 neighbouring positions
- qkv_weight: float32 [768, 3, 768], P('dp', None, 'tensor'), may hold values from -0.21875 to 0.21875
- out_weight: float32 [768, 768], P('dp', 'tensor'), may hold values from -0.875 to 0.875
- gateup_weight: float32 [768, 2, 3072], P('dp', None, 'tensor'), may hold values from -0.21875 to 0.21875
- down_weight: float32 [768, 3072], P('dp', 'tensor'), may hold values from -0.21875 to 0.21875
- norm_gains: float32 [768, 2], P('dp'), may hold values from 0.5 to 1.5
- qkv_momentum: float32 [768, 3, 768], P('dp', None, 'tensor'), may hold values from -64 to 64
- out_momentum: float32 [768, 768], P('dp', 'tensor'), may hold values from -64 to 64
- gateup_momentum: float32 [768, 2, 3072], P('dp', None, 'tensor'), may hold values from -64 to 64
- down_momentum: float32 [768, 3072], P('dp', 'tensor'), may hold values from -64 to 64
- gains_momentum: float32 [768, 2], P('dp'), may hold values from -64 to 64
- qkv_average: float32 [768, 3, 768], P('dp', None, 'tensor'), may hold values from -0.21875 to 0.21875
- out_average: float32 [768, 768], P('dp', 'tensor'), may hold values from -0.875 to 0.875
- gateup_average: float32 [768, 2, 3072], P('dp', None, 'tensor'), may hold values from -0.21875 to 0.21875
- down_average: float32 [768, 3072], P('dp', 'tensor'), may hold values from -0.21875 to 0.21875
- gains_average: float32 [768, 2], P('dp'), may hold values from -0.5 to 0.5
Outputs:
- output: bfloat16 [2, 4096, 768], P(None, 'dp')
- input_grad: float32 [2, 4096, 768], P(None, 'dp')
- qkv_grad: float32 [768, 3, 768], P('dp', None, 'tensor')
- out_grad: float32 [768, 768], P('dp', 'tensor')
- gateup_grad: float32 [768, 2, 3072], P('dp', None, 'tensor')
- down_grad: float32 [768, 3072], P('dp', 'tensor')
- gains_grad: float32 [768, 2], P('dp')
- qkv_moment: float32 [768, 3, 768], P('dp', None, 'tensor')
- out_moment: float32 [768, 768], P('dp', 'tensor')
- gateup_moment: float32 [768, 2, 3072], P('dp', None, 'tensor')
- down_moment: float32 [768, 3072], P('dp', 'tensor')
- gains_moment: float32 [768, 2], P('dp')
- qkv_updated: float32 [768, 3, 768], P('dp', None, 'tensor')
- out_updated: float32 [768, 768], P('dp', 'tensor')
- gateup_updated: float32 [768, 2, 3072], P('dp', None, 'tensor')
- down_updated: float32 [768, 3072], P('dp', 'tensor')
- gains_updated: float32 [768, 2], P('dp')
- qkv_averaged: float32 [768, 3, 768], P('dp', None, 'tensor')
- out_averaged: float32 [768, 768], P('dp', 'tensor')
- gateup_averaged: float32 [768, 2, 3072], P('dp', None, 'tensor')
- down_averaged: float32 [768, 3072], P('dp', 'tensor')
- gains_averaged: float32 [768, 2], P('dp')
The draws below stay inside these ranges and needn't reach their ends.
Inputs may be any that keep to these rules, and one draw needn't show every extreme that they name: `segments`: along each sequence the document numbers never fall; every document has 1 to 512 tokens and one document of each sequence has exactly 512.
All inputs are finite; a program needn't handle non-finite values.
Results may differ from the reference program's by a relative error of at most 0.015.
The reference program's roundings to bfloat16 on the way count: a program that leaves them out, or rounds other values in their place, can miss the bound.
Values may be sent and summed in bfloat16 or wider, within the bound.
No kernel may reach another device: no remote copies, remote signals or barrier semaphores. Data moves between devices by JAX's collectives and lax.ppermute only.
A program may use at most 128 MiB of HBM per device.

```python
import math
from functools import partial
import jax
import jax.numpy as jnp
import numpy as np
from jax import lax

D = 768
HEADS = 12
HEAD_DIM = 64
FF = 3072
TOK_DEV = 256
MICRO = 2
REACH = 2
TOKENS = 4096
DOC_MOST = 512
DOCS = 32


def steps_of(own_key, shape, pieces, smallest, largest):
    def one(dim, parts):
        draws = jax.random.uniform(jax.random.fold_in(jax.random.fold_in(own_key, 6), dim), (parts,), jnp.float32, smallest / len(pieces), largest / len(pieces))
        return jnp.repeat(jnp.exp(draws), shape[dim] // parts).reshape((-1,) + (1,) * (len(shape) - dim - 1))

    factor_of = one(*pieces[0])
    for cut in pieces[1:]:
        factor_of = factor_of * one(*cut)
    return factor_of


def profile(count, total, most, lean):
    loads = [(1 << 20) // math.isqrt(grade ** lean) + 1 for grade in range(2, count + 1)]
    spare, counts = total - most - (count - 1), [1] * (count - 1)
    while spare > 0:
        movable = [i for i in range(count - 1) if counts[i] < most]
        whole, budget = sum([loads[i] for i in movable]), spare
        for i in movable:
            extra = min(most - counts[i], max(1, budget * loads[i] // whole), spare)
            counts[i] = counts[i] + extra
            spare = spare - extra
    return np.array([most] + counts)


def uneven_parts(own_key, count, total, bound, skew):
    if count == 2:
        one = jax.random.randint(own_key, (), max(1, total - bound), min(bound, total - 1) + 1)
        return jnp.stack([one, total - one])
    lengths = jnp.asarray(profile(count, total, bound, skew), jnp.int32)
    twos = (count - 1) // 2
    giver, receiver = lengths[1:1 + 2 * twos:2], lengths[2:2 + 2 * twos:2]
    margin = jnp.minimum(giver - 1, bound - receiver)
    passed = jax.random.randint(jax.random.fold_in(own_key, 1), (twos,), 0, 1 << 20) % (margin + 1)
    lengths = lengths.at[1:1 + 2 * twos:2].set(giver - passed).at[2:2 + 2 * twos:2].set(receiver + passed)
    return lengths[jax.random.permutation(jax.random.fold_in(own_key, 2), count)]


def gaussian(stream_key, shape, deviation, bound, cuts=(), kind=jnp.bfloat16):
    factor_of = steps_of(stream_key, shape, cuts, -0.22, 0.18) if cuts else 1.0
    entries = jax.random.normal(stream_key, shape, jnp.float32) * deviation * factor_of
    return jnp.minimum(jnp.maximum(entries, -bound), bound).astype(kind)


def setup_inputs(seed: int = 0) -> dict:
    key_of = jax.random.split(jax.random.key(seed), 19)
    inputs = gaussian(key_of[0], (MICRO, TOKENS, D), 1.0, 6.0, ((1, 16),))
    cotangent = gaussian(key_of[1], (MICRO, TOKENS, D), 1.0, 6.0, ((1, 16),))
    segments = jax.vmap(lambda own: jnp.searchsorted(jnp.cumsum(uneven_parts(own, DOCS, TOKENS, DOC_MOST, 2)), jnp.arange(TOKENS), side="right"))(jax.random.split(key_of[2], MICRO)).reshape((MICRO, TOKENS)).astype(jnp.int32)
    qkv_weight = gaussian(key_of[3], (D, 3, D), D ** -0.5, 0.21875, ((0, 16), (2, 2)), jnp.float32)
    out_weight = gaussian(key_of[4], (D, D), (D // 16) ** -0.5, 0.875, ((0, 16), (1, 2)), jnp.float32)
    gateup_weight = gaussian(key_of[5], (D, 2, FF), D ** -0.5, 0.21875, ((0, 16), (2, 2)), jnp.float32)
    down_weight = gaussian(key_of[6], (D, FF), (FF // 4) ** -0.5, 0.21875, ((0, 16), (1, 2)), jnp.float32)
    norm_gains = jnp.clip(1.0 + 0.1 * jax.random.normal(key_of[7], (D, 2), jnp.float32), 0.5, 1.5)
    qkv_momentum = gaussian(key_of[8], (D, 3, D), 10.0, 64.0, ((0, 16), (2, 2)), jnp.float32)
    out_momentum = gaussian(key_of[9], (D, D), 10.0, 64.0, ((0, 16), (1, 2)), jnp.float32)
    gateup_momentum = gaussian(key_of[10], (D, 2, FF), 10.0, 64.0, ((0, 16), (2, 2)), jnp.float32)
    down_momentum = gaussian(key_of[11], (D, FF), 10.0, 64.0, ((0, 16), (1, 2)), jnp.float32)
    gains_momentum = gaussian(key_of[12], (D, 2), 10.0, 64.0, ((0, 16),), jnp.float32)
    qkv_average = gaussian(key_of[13], (D, 3, D), D ** -0.5, 0.21875, ((0, 16), (2, 2)), jnp.float32)
    out_average = gaussian(key_of[14], (D, D), (D // 16) ** -0.5, 0.875, ((0, 16), (1, 2)), jnp.float32)
    gateup_average = gaussian(key_of[15], (D, 2, FF), D ** -0.5, 0.21875, ((0, 16), (2, 2)), jnp.float32)
    down_average = gaussian(key_of[16], (D, FF), (FF // 4) ** -0.5, 0.21875, ((0, 16), (1, 2)), jnp.float32)
    gains_average = jnp.clip(jax.random.uniform(key_of[17], (D, 2), jnp.float32, -0.5, 0.5) * steps_of(key_of[17], (D, 2), ((0, 16),), -0.4, 0.0), -0.5, 0.5)
    return {"inputs": inputs, "cotangent": cotangent, "segments": segments, "qkv_weight": qkv_weight, "out_weight": out_weight, "gateup_weight": gateup_weight, "down_weight": down_weight, "norm_gains": norm_gains, "qkv_momentum": qkv_momentum, "out_momentum": out_momentum, "gateup_momentum": gateup_momentum, "down_momentum": down_momentum, "gains_momentum": gains_momentum, "qkv_average": qkv_average, "out_average": out_average, "gateup_average": gateup_average, "down_average": down_average, "gains_average": gains_average}


NORM_EPS = 1e-05
ROPE_BASE = 10000.0
MOMENTUM = 0.9
LEARN_RATE = 0.0003
AVERAGE_RATE = 0.9
MASKED = -1e+30

@jax.custom_vjp
def low(v):
    return lax.optimization_barrier(v.astype(jnp.bfloat16)).astype(jnp.float32)

@jax.custom_vjp
def low_back(v):
    return v

def low_keep(v):
    return (low(v), None)

def low_pass(kept, grad):
    return (grad,)

def back_keep(v):
    return (v, None)

def back_low(kept, grad):
    return (low(grad),)
low.defvjp(low_keep, low_pass)
low_back.defvjp(back_keep, back_low)

def rotate_half(values):
    half = values.shape[-1] // 2
    return jnp.concatenate([-values[..., half:], values[..., :half]], axis=-1)

def rope_tables(first, count):
    position = (first + jnp.arange(count, dtype=jnp.int32)).astype(jnp.float32)
    inverse = ROPE_BASE ** (-jnp.arange(0, HEAD_DIM, 2, dtype=jnp.float32) / HEAD_DIM)
    angles = position[:, None] * inverse[None, :]
    angles = jnp.concatenate([angles, angles], axis=-1)
    return (jnp.cos(angles)[:, None, :], jnp.sin(angles)[:, None, :])

def apply_rope(values, cosine, sine):
    return values * cosine + rotate_half(values) * sine

def rms_normed(values, gain):
    scale_inv = lax.rsqrt(lax.optimization_barrier(jnp.mean(values * values, axis=-1, keepdims=True)) + NORM_EPS)
    return low(values * scale_inv * gain)

def attention(queries, keys_all, values_all, seg_row):
    length = queries.shape[0]
    pad_rows = REACH * TOK_DEV
    span = (REACH + 1) * TOK_DEV
    keys_pad = jnp.concatenate([jnp.zeros((pad_rows,) + keys_all.shape[1:], keys_all.dtype), keys_all], axis=0)
    values_pad = jnp.concatenate([jnp.zeros((pad_rows,) + values_all.shape[1:], values_all.dtype), values_all], axis=0)
    seg_pad = jnp.concatenate([jnp.full((pad_rows,), -1, jnp.int32), seg_row.astype(jnp.int32)])

    def block(number):
        start = (number * TOK_DEV).astype(jnp.int32)
        q_block = lax.dynamic_slice_in_dim(queries, start, TOK_DEV, 0)
        k_block = lax.dynamic_slice_in_dim(keys_pad, start, span, 0)
        v_block = lax.dynamic_slice_in_dim(values_pad, start, span, 0)
        seg_query = lax.dynamic_slice_in_dim(seg_row.astype(jnp.int32), start, TOK_DEV, 0)
        seg_keys = lax.dynamic_slice_in_dim(seg_pad, start, span, 0)
        query_pos = jnp.arange(TOK_DEV, dtype=jnp.int32)[:, None] + pad_rows
        key_pos = jnp.arange(span, dtype=jnp.int32)[None, :]
        visible = (seg_query[:, None] == seg_keys[None, :]) & (key_pos <= query_pos)
        scores = low_back(jnp.einsum('qhe,khe->hqk', q_block, k_block, precision=lax.Precision.HIGHEST) * HEAD_DIM ** (-0.5))
        scores = jnp.where(visible[None], scores, MASKED)
        probs = low(jax.nn.softmax(scores, axis=-1))
        return jnp.einsum('hqk,khe->qhe', probs, v_block, precision=lax.Precision.HIGHEST)
    blocks = lax.map(jax.checkpoint(block), jnp.arange(length // TOK_DEV, dtype=jnp.int32))
    return blocks.reshape(length, HEADS * HEAD_DIM)

def forward(qkv_weight, out_weight, gateup_weight, down_weight, norm_gains, tokens, seg_row):
    qkv_w = low(qkv_weight)
    out_w = low(out_weight)
    gateup_w = low(gateup_weight)
    down_w = low(down_weight)
    gain_w = low(norm_gains)
    length = tokens.shape[0]
    normed_one = rms_normed(tokens, gain_w[:, 0])
    mixed = jnp.einsum('td,dch->tch', normed_one, qkv_w, precision=lax.Precision.HIGHEST)
    cosine, sine = rope_tables(0, length)
    query_pre = low_back(mixed[:, 0]).reshape(length, HEADS, HEAD_DIM)
    key_pre = low_back(mixed[:, 1]).reshape(length, HEADS, HEAD_DIM)
    queries = low(apply_rope(query_pre, cosine, sine))
    keys_all = low(apply_rope(key_pre, cosine, sine))
    values_all = low(low_back(mixed[:, 2])).reshape(length, HEADS, HEAD_DIM)
    attended = low(low_back(attention(queries, keys_all, values_all, seg_row)))
    branch = low_back(jnp.einsum('th,dh->td', attended, out_w, precision=lax.Precision.HIGHEST))
    resid = tokens + branch
    normed_two = rms_normed(resid, gain_w[:, 1])
    gateup = jnp.einsum('td,dcf->tcf', normed_two, gateup_w, precision=lax.Precision.HIGHEST)
    gate = low_back(gateup[:, 0])
    upward = low_back(gateup[:, 1])
    hidden = low(jax.nn.silu(gate) * upward)
    return resid + jnp.einsum('tf,df->td', hidden, down_w, precision=lax.Precision.HIGHEST)

def reference(inputs, cotangent, segments, qkv_weight, out_weight, gateup_weight, down_weight, norm_gains, qkv_momentum, out_momentum, gateup_momentum, down_momentum, gains_momentum, qkv_average, out_average, gateup_average, down_average, gains_average):
    masters = (qkv_weight, out_weight, gateup_weight, down_weight, norm_gains)
    totals = tuple((jnp.zeros_like(master) for master in masters))
    results = []
    input_grads = []
    for index in range(MICRO):
        tokens = inputs[index].astype(jnp.float32)
        primal, pullback = jax.vjp(partial(forward, seg_row=segments[index]), *masters, tokens)
        pulled = pullback(cotangent[index].astype(jnp.float32))
        totals = tuple((total + piece for total, piece in zip(totals, pulled[:5])))
        results.append(primal.astype(jnp.bfloat16))
        input_grads.append(pulled[5])
    moments = (qkv_momentum, out_momentum, gateup_momentum, down_momentum, gains_momentum)
    averages = (qkv_average, out_average, gateup_average, down_average, gains_average)
    new_moments = tuple((MOMENTUM * previous + gradient for previous, gradient in zip(moments, totals)))
    updated = tuple((master - LEARN_RATE * (gradient + MOMENTUM * moment) for master, gradient, moment in zip(masters, totals, new_moments)))
    averaged = tuple((AVERAGE_RATE * previous + (1.0 - AVERAGE_RATE) * weight for previous, weight in zip(averages, updated)))
    output = jnp.stack(results)
    input_grad = jnp.stack(input_grads)
    return (output, input_grad, totals[0], totals[1], totals[2], totals[3], totals[4], new_moments[0], new_moments[1], new_moments[2], new_moments[3], new_moments[4], updated[0], updated[1], updated[2], updated[3], updated[4], averaged[0], averaged[1], averaged[2], averaged[3], averaged[4])
```

```python
import jax
import jax.numpy as jnp
from jax import lax
from jax.sharding import PartitionSpec as P

HEAD_DIM = 64
REACH = 2

NORM_EPS = 1e-05
ROPE_BASE = 10000.0
MOMENTUM = 0.9
LEARN_RATE = 0.0003
AVERAGE_RATE = 0.9
MASKED = -1e30


BF = jnp.bfloat16
F32 = jnp.float32


def dot(left, right, contract):
    return lax.dot_general(left, right, (contract, ((), ())), preferred_element_type=F32)


def ring_chip(place, chips):
    return jnp.where(place < chips // 2, 2 * place, 2 * (chips - 1 - place) + 1)


def ring_place(chip, chips):
    return jnp.where(chip % 2 == 0, chip // 2, chips - 1 - chip // 2)


def ring_pairs(count):
    chips = count // 2
    order = [2 * i for i in range(chips // 2)] + [
        2 * (chips - 1 - i) + 1 for i in range(chips // 2, chips)
    ]
    onward = [
        (2 * order[i] + core, 2 * order[(i + 1) % chips] + core)
        for i in range(chips)
        for core in range(2)
    ]
    return onward, [(b, a) for a, b in onward]


def core_swap(value):
    count = lax.axis_size("dp")
    return lax.ppermute(value, "dp", [(i, i ^ 1) for i in range(count)])


def tensor_swap(value):
    count = lax.axis_size("tensor")
    return lax.ppermute(value, "tensor", [(i, i ^ 1) for i in range(count)])


def tensor_sum(part):
    low = part.astype(BF)
    return low.astype(F32) + tensor_swap(low).astype(F32)


def feature_order(rows):
    count = lax.axis_size("dp")
    chips = count // 2
    rank = lax.axis_index("dp")
    core = rank % 2
    place = ring_place(rank // 2, chips)
    index = jnp.arange(count * rows, dtype=jnp.int32)
    group = index // (chips * rows)
    inside = index % (chips * rows)
    distance = inside // rows
    row = inside % rows
    ahead = jnp.where(row < rows // 2, -distance, distance)
    chip = ring_chip((place + ahead + chips) % chips, chips)
    return (2 * chip + jnp.where(group == 0, core, 1 - core)) * rows + row


def ring_gather(shard):
    count = lax.axis_size("dp")
    onward, back = ring_pairs(count)
    half = shard.shape[0] // 2
    lower, upper = shard[:half], shard[half:]
    parts = [shard]
    for _ in range(count // 2 - 1):
        lower = lax.ppermute(lower, "dp", onward)
        upper = lax.ppermute(upper, "dp", back)
        parts += [lower, upper]
    mine = jnp.concatenate(parts, axis=0)
    return jnp.concatenate([mine, core_swap(mine)], axis=0)


def ring_scatter(mine, theirs, rows):
    count = lax.axis_size("dp")
    onward, back = ring_pairs(count)
    half = rows // 2
    other = core_swap(theirs)

    def piece(distance, side):
        first = distance * rows + side * half
        return mine[first : first + half] + other[first : first + half].astype(F32)

    last = count // 2 - 1
    lower, upper = piece(last, 0), piece(last, 1)
    for distance in range(last - 1, -1, -1):
        lower = lax.ppermute(lower.astype(BF), "dp", back).astype(F32) + piece(distance, 0)
        upper = lax.ppermute(upper.astype(BF), "dp", onward).astype(F32) + piece(distance, 1)
    return jnp.concatenate([lower, upper], axis=0)


def rotate_half(values):
    half = HEAD_DIM // 2
    lane = lax.broadcasted_iota(jnp.int32, values.shape, 1) % HEAD_DIM
    ahead = jnp.concatenate([values[:, half:], values[:, :half]], axis=1)
    behind = jnp.concatenate([values[:, -half:], values[:, :-half]], axis=1)
    return jnp.where(lane < half, -ahead, behind)


def rope_tables(first, count, heads):
    position = (first + jnp.arange(count, dtype=jnp.int32)).astype(F32)
    inverse = ROPE_BASE ** (-jnp.arange(0, HEAD_DIM, 2, dtype=F32) / HEAD_DIM)
    angles = position[:, None] * inverse[None, :]
    angles = jnp.concatenate([angles, angles] * heads, axis=-1)
    return jnp.cos(angles), jnp.sin(angles)


def norm_forward(values, gain):
    scale_inv = lax.rsqrt(jnp.mean(values * values, axis=-1, keepdims=True) + NORM_EPS)
    unit = values * scale_inv
    return scale_inv, unit, (unit * gain).astype(BF)


def norm_backward(scale_inv, unit, gain, upstream):
    weighted = upstream * gain
    inner = jnp.mean(weighted * unit, axis=-1, keepdims=True)
    return scale_inv * (weighted - unit * inner)


def by_head(values):
    return values.reshape(values.shape[0], -1, HEAD_DIM)


def body(
    inputs,
    cotangent,
    segments,
    qkv_weight,
    out_weight,
    gateup_weight,
    down_weight,
    norm_gains,
    qkv_momentum,
    out_momentum,
    gateup_momentum,
    down_momentum,
    gains_momentum,
    qkv_average,
    out_average,
    gateup_average,
    down_average,
    gains_average,
):
    masters = (qkv_weight, out_weight, gateup_weight, down_weight, norm_gains)
    micro, count, model = inputs.shape
    rows = qkv_weight.shape[0]
    width = qkv_weight.shape[2]
    hidden_units = down_weight.shape[1]
    heads = width // HEAD_DIM
    span = (REACH + 1) * count
    devices = lax.axis_size("dp")
    rank = lax.axis_index("dp")
    core = rank % 2
    side = lax.axis_index("tensor")
    scale = HEAD_DIM ** (-0.5)

    gain_columns = jnp.pad(norm_gains.astype(BF), ((0, 0), (0, 126)))
    first_group = jnp.concatenate(
        [
            qkv_weight.reshape(rows, 3 * width).astype(BF),
            out_weight.astype(BF),
            gain_columns,
        ],
        axis=1,
    )
    second_group = jnp.concatenate(
        [gateup_weight.reshape(rows, 2 * hidden_units).astype(BF), down_weight.astype(BF)],
        axis=1,
    )
    onward_chip = [(i, i + 2) for i in range(devices - 2)]
    fetched = lax.ppermute(
        lax.dynamic_index_in_dim(inputs, side, 0, keepdims=False), "dp", onward_chip
    )
    swapped = tensor_swap(fetched)
    two_back = jnp.stack(
        [jnp.where(side == 0, fetched, swapped), jnp.where(side == 0, swapped, fetched)]
    )
    one_back = core_swap(jnp.where(core == 0, inputs, two_back))

    whole_one = ring_gather(first_group)
    whole_two = ring_gather(second_group)
    order = feature_order(rows)
    select = (jnp.arange(model, dtype=jnp.int32)[:, None] == order[None, :]).astype(BF)
    qkv_full = whole_one[:, : 3 * width]
    out_full = whole_one[:, 3 * width : 4 * width]
    gains_row = whole_one[:, 4 * width : 4 * width + 8].T.astype(F32)
    gain_one, gain_two = gains_row[0:1], gains_row[1:2]
    gateup_full = whole_two[:, : 2 * hidden_units]
    down_full = whole_two[:, 2 * hidden_units :]

    padded = jnp.concatenate([jnp.full((micro, REACH * count), -1, jnp.int32), segments], axis=1)
    start = rank * count
    seg_keys = lax.dynamic_slice_in_dim(padded, start, span, 1)
    seg_query = lax.dynamic_slice_in_dim(segments, start, count, 1)
    query_pos = jnp.arange(count, dtype=jnp.int32)[:, None] + REACH * count
    key_pos = jnp.arange(span, dtype=jnp.int32)[None, :]
    cosine, sine = rope_tables(start - REACH * count, span, heads)
    cos_own, sin_own = cosine[REACH * count :], sine[REACH * count :]

    def attention_forward(index):
        raw = jnp.concatenate([two_back[index], one_back[index], inputs[index]], axis=0)
        ordered = dot(raw, select, ((1,), (0,)))
        scale_one, unit_one, normed = norm_forward(ordered, gain_one)
        own = normed[REACH * count :]
        pre_q = dot(own, qkv_full[:, :width], ((1,), (0,)))
        pre_kv = dot(normed, qkv_full[:, width:], ((1,), (0,)))
        pre_k = pre_kv[:, :width]
        queries = by_head((pre_q * cos_own + rotate_half(pre_q) * sin_own).astype(BF))
        keys = by_head((pre_k * cosine + rotate_half(pre_k) * sine).astype(BF))
        values = by_head(pre_kv[:, width:].astype(BF))
        visible = (seg_query[index][:, None] == seg_keys[index][None, :]) & (key_pos <= query_pos)
        scores = jnp.einsum("qhe,khe->hqk", queries, keys, preferred_element_type=F32)
        scores = jnp.where(visible[None], scores * scale, MASKED)
        peak = jnp.max(scores, axis=-1, keepdims=True)
        expon = jnp.exp(scores - peak)
        totals = jnp.sum(expon, axis=-1, keepdims=True)
        log_total = peak + jnp.log(totals)
        probs_low = (expon / totals).astype(BF)
        attended = jnp.einsum("hqk,khe->qhe", probs_low, values, preferred_element_type=F32)
        attended = attended.reshape(count, width).astype(BF)
        branch = tensor_sum(dot(attended, out_full, ((1,), (1,))))
        return dict(
            x=ordered[REACH * count :],
            s1=scale_one[REACH * count :],
            h1=unit_one[REACH * count :],
            n1=own,
            q=queries,
            k=keys,
            v=values,
            vis=visible,
            lse=log_total,
            ob=attended,
            branch=branch,
        )

    def feed_forward(index, kept):
        resid = kept["x"] + kept["branch"]
        scale_two, unit_two, normed = norm_forward(resid, gain_two)
        upstream = dot(cotangent[index], select, ((1,), (0,))).astype(BF)
        gateup = dot(normed, gateup_full, ((1,), (0,)))
        gate, upward = gateup[:, :hidden_units], gateup[:, hidden_units:]
        sigma = jax.nn.sigmoid(gate)
        active = gate * sigma
        hidden = (active * upward).astype(BF)
        down = tensor_sum(dot(hidden, down_full, ((1,), (1,))))
        result = (resid + down).astype(BF)
        grad_hidden = dot(upstream, down_full, ((1,), (0,)))
        grad_gate = (grad_hidden * upward * sigma * (1.0 + gate * (1.0 - sigma))).astype(BF)
        grad_up = (grad_hidden * active).astype(BF)
        grad_gateup = jnp.concatenate([grad_gate, grad_up], axis=1)
        grad_normed = tensor_sum(dot(grad_gateup, gateup_full, ((1,), (1,))))
        grad_resid = upstream.astype(F32) + norm_backward(
            scale_two, unit_two, gain_two, grad_normed
        )
        gain_term = jnp.sum(unit_two * grad_normed, axis=0)
        return dict(
            result=dot(result, select, ((1,), (1,))).astype(BF),
            dy=upstream,
            n2=normed,
            hid=hidden,
            dgu=grad_gateup,
            dr1=grad_resid,
            da=grad_resid.astype(BF),
            gain=gain_term,
        )

    def attention_backward(index, kept, later):
        grad_heads = by_head(dot(later["da"], out_full, ((1,), (0,))).astype(BF))
        queries, keys, values = kept["q"], kept["k"], kept["v"]
        scores = jnp.einsum("qhe,khe->hqk", queries, keys, preferred_element_type=F32)
        scores = jnp.where(kept["vis"][None], scores * scale, MASKED)
        probs = jnp.exp(scores - kept["lse"])
        grad_probs = jnp.einsum("qhe,khe->hqk", grad_heads, values, preferred_element_type=F32)
        inner = jnp.sum(probs * grad_probs, axis=-1, keepdims=True)
        grad_scores = (probs * (grad_probs - inner)).astype(BF)
        grad_q = jnp.einsum("hqk,khe->qhe", grad_scores, keys, preferred_element_type=F32) * scale
        grad_k = (
            jnp.einsum("hqk,qhe->khe", grad_scores, queries, preferred_element_type=F32) * scale
        )
        grad_v = jnp.einsum(
            "hqk,qhe->khe", probs.astype(BF), grad_heads, preferred_element_type=F32
        )
        grad_kv = jnp.concatenate(
            [grad_k.reshape(span, width), grad_v.reshape(span, width)], axis=1
        )
        far, near, own = grad_kv[:count], grad_kv[count : 2 * count], grad_kv[2 * count :]
        from_core = core_swap(near.astype(BF)).astype(F32)
        own = own + jnp.where(core == 0, from_core, 0.0)
        sent = far + jnp.where(core == 0, 0.0, from_core)
        behind = [(i + 2, i) for i in range(devices - 2)]
        own = own + lax.ppermute(sent.astype(BF), "dp", behind).astype(F32)
        grad_q = grad_q.reshape(count, width)
        grad_q = grad_q * cos_own - rotate_half(grad_q * sin_own)
        grad_k = own[:, :width]
        grad_k = grad_k * cos_own - rotate_half(grad_k * sin_own)
        grad_mixed = jnp.concatenate([grad_q, grad_k, own[:, width:]], axis=1).astype(BF)
        part = dot(grad_mixed, qkv_full, ((1,), (1,)))
        gain_term = jnp.sum(kept["h1"] * part, axis=0)
        grad_normed = tensor_sum(part)
        grad_tokens = later["dr1"] + norm_backward(
            kept["s1"], kept["h1"], gain_one, grad_normed
        )
        grad_tokens = lax.dot_general(
            grad_tokens,
            select.astype(F32),
            (((1,), (1,)), ((), ())),
            precision=lax.Precision.HIGHEST,
            preferred_element_type=F32,
        )
        return dict(dx=grad_tokens, dmix=grad_mixed, gain=gain_term)

    ahead = [attention_forward(i) for i in range(micro)]
    ffn = [feed_forward(i, ahead[i]) for i in range(micro)]

    def join(source, name):
        return jnp.concatenate([item[name] for item in source], axis=0)

    split = model // 2

    def weight_grads(pairs):
        mine = [dot(left[:, :split], right, ((0,), (0,))) for left, right in pairs]
        theirs = [dot(left[:, split:], right, ((0,), (0,))).astype(BF) for left, right in pairs]
        return mine, theirs

    mine, theirs = weight_grads(
        [(join(ffn, "n2"), join(ffn, "dgu")), (join(ffn, "dy"), join(ffn, "hid"))]
    )
    reduced_two = ring_scatter(
        jnp.concatenate(mine, axis=1), jnp.concatenate(theirs, axis=1), rows
    )
    back = [attention_backward(i, ahead[i], ffn[i]) for i in range(micro)]
    mine, theirs = weight_grads(
        [(join(ahead, "n1"), join(back, "dmix")), (join(ffn, "da"), join(ahead, "ob"))]
    )
    gain_terms = jnp.stack([back[0]["gain"], 0.5 * ffn[0]["gain"]], axis=1)
    for index in range(1, micro):
        gain_terms = gain_terms + jnp.stack(
            [back[index]["gain"], 0.5 * ffn[index]["gain"]], axis=1
        )
    gain_terms = jnp.pad(gain_terms, ((0, 0), (0, 126)))
    reduced_one = ring_scatter(
        jnp.concatenate(mine + [gain_terms[:split]], axis=1),
        jnp.concatenate(theirs + [gain_terms[split:].astype(BF)], axis=1),
        rows,
    )
    gains_part = reduced_one[:, 4 * width : 4 * width + 2]
    totals = (
        reduced_one[:, : 3 * width].reshape(rows, 3, width),
        reduced_one[:, 3 * width : 4 * width],
        reduced_two[:, : 2 * hidden_units].reshape(rows, 2, hidden_units),
        reduced_two[:, 2 * hidden_units :],
        gains_part + tensor_swap(gains_part),
    )
    moments = (qkv_momentum, out_momentum, gateup_momentum, down_momentum, gains_momentum)
    averages = (qkv_average, out_average, gateup_average, down_average, gains_average)
    new_moments = tuple(
        (MOMENTUM * previous + gradient for previous, gradient in zip(moments, totals))
    )
    updated = tuple(
        (
            master - LEARN_RATE * (gradient + MOMENTUM * moment)
            for master, gradient, moment in zip(masters, totals, new_moments)
        )
    )
    averaged = tuple(
        (
            AVERAGE_RATE * previous + (1.0 - AVERAGE_RATE) * weight
            for previous, weight in zip(averages, updated)
        )
    )
    return (
        (jnp.stack([f["result"] for f in ffn]), jnp.stack([b["dx"] for b in back]))
        + tuple(totals)
        + new_moments
        + updated
        + averaged
    )


def solution(mesh):
    tokens = P(None, "dp", None)
    shards = (
        P("dp", None, "tensor"),
        P("dp", "tensor"),
        P("dp", None, "tensor"),
        P("dp", "tensor"),
        P("dp", None),
    )
    return jax.shard_map(
        body,
        mesh=mesh,
        in_specs=(tokens, tokens, P()) + shards * 3,
        out_specs=(tokens, tokens) + shards * 4,
        check_vma=False,
    )
```

```python
from functools import partial

import jax
import jax.numpy as jnp
from jax import lax
from jax.experimental import pallas as pl
from jax.experimental.pallas import tpu as pltpu
from jax.sharding import PartitionSpec as P

HEAD_DIM = 64
REACH = 2

NORM_EPS = 1e-05
ROPE_BASE = 10000.0
MOMENTUM = 0.9
LEARN_RATE = 0.0003
AVERAGE_RATE = 0.9
MASKED = -1e30
LANES = 128
FFN_STEP = 512
GRAD_STEP = 768


BF = jnp.bfloat16
F32 = jnp.float32


def dot(left, right, contract):
    return lax.dot_general(left, right, (contract, ((), ())), preferred_element_type=F32)


def ring_chip(place, chips):
    return jnp.where(place < chips // 2, 2 * place, 2 * (chips - 1 - place) + 1)


def ring_place(chip, chips):
    return jnp.where(chip % 2 == 0, chip // 2, chips - 1 - chip // 2)


def ring_pairs(count):
    chips = count // 2
    order = [2 * i for i in range(chips // 2)] + [
        2 * (chips - 1 - i) + 1 for i in range(chips // 2, chips)
    ]
    onward = [
        (2 * order[i] + core, 2 * order[(i + 1) % chips] + core)
        for i in range(chips)
        for core in range(2)
    ]
    return onward, [(b, a) for a, b in onward]


def core_swap(value):
    count = lax.axis_size("dp")
    return lax.ppermute(value, "dp", [(i, i ^ 1) for i in range(count)])


def tensor_swap(value):
    count = lax.axis_size("tensor")
    return lax.ppermute(value, "tensor", [(i, i ^ 1) for i in range(count)])


def feature_order(rows):
    count = lax.axis_size("dp")
    chips = count // 2
    rank = lax.axis_index("dp")
    core = rank % 2
    place = ring_place(rank // 2, chips)
    index = jnp.arange(count * rows, dtype=jnp.int32)
    group = index // (chips * rows)
    inside = index % (chips * rows)
    distance = inside // rows
    row = inside % rows
    ahead = jnp.where(row < rows // 2, -distance, distance)
    chip = ring_chip((place + ahead + chips) % chips, chips)
    return (2 * chip + jnp.where(group == 0, core, 1 - core)) * rows + row


class RingGather:
    def __init__(self, shard):
        half = shard.shape[0] // 2
        self.flight = (shard[:half], shard[half:])
        self.parts = [shard]
        self.left = lax.axis_size("dp") // 2 - 1
        self.launch()

    def launch(self):
        onward, back = ring_pairs(lax.axis_size("dp"))
        lower, upper = self.flight
        self.flight = (lax.ppermute(lower, "dp", onward), lax.ppermute(upper, "dp", back))

    def step(self, beside=()):
        if self.left == 0:
            return beside
        self.flight, beside = lax.optimization_barrier((self.flight, beside))
        self.parts += list(self.flight)
        self.left -= 1
        if self.left:
            self.launch()
        return beside

    def finish(self):
        while self.left:
            self.step()
        mine = jnp.concatenate(self.parts, axis=0)
        return jnp.concatenate([mine, core_swap(mine)], axis=0)


class RingScatter:
    def __init__(self, mine, theirs, rows):
        self.mine, self.rows = mine, rows
        self.other = core_swap(theirs)
        self.left = lax.axis_size("dp") // 2 - 1
        self.sums = (self.piece(self.left, 0), self.piece(self.left, 1))
        self.launch()

    def piece(self, distance, side):
        half = self.rows // 2
        first = distance * self.rows + side * half
        return self.mine[first : first + half] + self.other[first : first + half].astype(F32)

    def launch(self):
        onward, back = ring_pairs(lax.axis_size("dp"))
        lower, upper = self.sums
        self.flight = (
            lax.ppermute(lower.astype(BF), "dp", back),
            lax.ppermute(upper.astype(BF), "dp", onward),
        )

    def step(self, beside=()):
        if self.left == 0:
            return beside
        self.flight, beside = lax.optimization_barrier((self.flight, beside))
        self.left -= 1
        self.sums = tuple(
            flown.astype(F32) + self.piece(self.left, side)
            for side, flown in enumerate(self.flight)
        )
        if self.left:
            self.launch()
        return beside

    def finish(self):
        while self.left:
            self.step()
        return jnp.concatenate(self.sums, axis=0)


def rope_tables(first, count):
    position = (first + jnp.arange(count, dtype=jnp.int32)).astype(F32)
    inverse = ROPE_BASE ** (-jnp.arange(0, HEAD_DIM, 2, dtype=F32) / HEAD_DIM)
    angles = position[:, None] * inverse[None, :]
    angles = jnp.concatenate([angles] * (LANES // (HEAD_DIM // 2)), axis=-1)
    return jnp.cos(angles), jnp.sin(angles)


def rotate_half(values):
    half = HEAD_DIM // 2
    lane = lax.broadcasted_iota(jnp.int32, values.shape, 1) % HEAD_DIM
    ahead = pltpu.roll(values, LANES - half, 1)
    behind = pltpu.roll(values, half, 1)
    return jnp.where(lane < half, -ahead, behind)


def rope(values, cosine, sine):
    return values * cosine + rotate_half(values) * sine


def unrope(gradient, cosine, sine):
    return gradient * cosine - rotate_half(gradient * sine)


def unit_norm(values):
    scale_inv = lax.rsqrt(jnp.mean(values * values, axis=-1, keepdims=True) + NORM_EPS)
    return scale_inv, values * scale_inv


def norm_backward(scale_inv, unit, gain, upstream):
    weighted = upstream * gain
    inner = jnp.mean(weighted * unit, axis=-1, keepdims=True)
    return scale_inv * (weighted - unit * inner)


def half_mask(values, half):
    lane = lax.broadcasted_iota(jnp.int32, values.shape, 1)
    return jnp.where(lane // HEAD_DIM == half, values, jnp.zeros_like(values))


def visible_of(key_seg, query_seg, count):
    shape = (key_seg.shape[0], query_seg.shape[1])
    key_pos = lax.broadcasted_iota(jnp.int32, shape, 0)
    query_pos = lax.broadcasted_iota(jnp.int32, shape, 1) + REACH * count
    return (key_seg == query_seg) & (key_pos <= query_pos)


def group(index):
    return pl.ds(pl.multiple_of(index * LANES, LANES), LANES)


def call(kernel, name, outs, *args, smem=0, limit=40):
    specs = [pl.BlockSpec(memory_space=pltpu.SMEM)] * smem
    specs += [pl.BlockSpec(memory_space=pltpu.VMEM)] * (len(args) - smem)
    return pl.pallas_call(
        kernel,
        name=name,
        out_shape=[jax.ShapeDtypeStruct(shape, kind) for shape, kind in outs],
        in_specs=specs,
        out_specs=[pl.BlockSpec(memory_space=pltpu.VMEM)] * len(outs),
        compiler_params=pltpu.CompilerParams(vmem_limit_bytes=limit * 1024 * 1024),
    )(*args)


def permute_kernel(order_ref, x_ref, dy_ref, select_ref, xp_ref, dyp_ref):
    model = x_ref.shape[-1]
    line = lax.broadcasted_iota(jnp.int32, (model, model), 0)
    select = (line == order_ref[...]).astype(F32).astype(BF)
    select_ref[...] = select
    for index in range(x_ref.shape[0]):
        xp_ref[index] = dot(x_ref[index], select, ((1,), (0,))).astype(BF)
        dyp_ref[index] = dot(dy_ref[index], select, ((1,), (0,))).astype(BF)


def halo_kernel(far_ref, near_ref, select_ref, out_ref):
    count = far_ref.shape[1]
    select = select_ref[...]
    for index in range(far_ref.shape[0]):
        out_ref[index, :count] = dot(far_ref[index], select, ((1,), (0,))).astype(BF)
        out_ref[index, count:] = dot(near_ref[index], select, ((1,), (0,))).astype(BF)


def qkv_kernel(x_ref, halo_ref, w_ref, cos_ref, sin_ref, n_ref, q_ref, k_ref, v_ref, gain_ref):
    count = x_ref.shape[0]
    width = q_ref.shape[1]
    gains = w_ref[:, 4 * width : 4 * width + LANES].astype(F32).T
    gain_ref[...] = gains[:8]
    gain = gains[0:1]
    blocks = REACH + 1
    for block in range(blocks):
        rows = slice(block * count, (block + 1) * count)
        own = block == REACH
        tokens = x_ref[...] if own else halo_ref[rows]
        _, unit = unit_norm(tokens.astype(F32))
        normed = (unit * gain).astype(BF)
        cosine, sine = cos_ref[rows], sin_ref[rows]
        keys = dot(normed, w_ref[:, width : 2 * width], ((1,), (0,)))
        v_ref[rows] = dot(normed, w_ref[:, 2 * width : 3 * width], ((1,), (0,))).astype(BF)
        for start in range(0, width, LANES):
            lanes = slice(start, start + LANES)
            k_ref[rows, lanes] = rope(keys[:, lanes], cosine, sine).astype(BF)
        if own:
            n_ref[...] = normed
            queries = dot(normed, w_ref[:, :width], ((1,), (0,)))
            for start in range(0, width, LANES):
                lanes = slice(start, start + LANES)
                turned = rope(queries[:, lanes], cosine, sine).astype(BF)
                q_ref[:, lanes] = turned * jnp.asarray(HEAD_DIM**-0.5, BF)


def attend_kernel(q_ref, k_ref, v_ref, keyseg_ref, queryseg_ref, w_ref, o_ref, lse_ref, a_ref):
    count, width = q_ref.shape
    visible = visible_of(keyseg_ref[...], queryseg_ref[...], count)

    def pair(index, _):
        lanes = group(index)
        queries, keys, values = q_ref[:, lanes], k_ref[:, lanes], v_ref[:, lanes]
        total = jnp.zeros((count, LANES), F32)
        for half in range(2):
            scores = dot(keys, half_mask(queries, half), ((1,), (1,)))
            scores = jnp.where(visible, scores, MASKED)
            peak = jnp.max(scores, axis=0, keepdims=True)
            expon = jnp.exp(scores - peak)
            sums = jnp.sum(expon, axis=0, keepdims=True)
            lse_ref[pl.ds(2 * index + half, 1), :] = peak + jnp.log(sums)
            probs = (expon * (1.0 / sums)).astype(BF)
            total = total + dot(probs, half_mask(values, half), ((0,), (0,)))
        o_ref[:, lanes] = total.astype(BF)
        return 0

    lax.fori_loop(0, width // LANES, pair, 0)
    out = w_ref[:, 3 * width : 4 * width]
    a_ref[...] = dot(o_ref[...], out, ((1,), (1,))).astype(BF)


def ffn_kernel(x_ref, a_ref, b_ref, dy_ref, gain_ref, w_ref, r_ref, n_ref, h_ref, d_ref, down_ref, dn_ref):
    hidden = h_ref.shape[1]
    resid = x_ref[...].astype(F32) + (a_ref[...].astype(F32) + b_ref[...].astype(F32))
    r_ref[...] = resid
    _, unit = unit_norm(resid)
    normed = (unit * gain_ref[1:2]).astype(BF)
    n_ref[...] = normed
    upstream = dy_ref[...]
    step = FFN_STEP
    down = jnp.zeros(resid.shape, F32)
    grad = jnp.zeros(resid.shape, F32)
    for first in range(0, hidden, step):
        g_cols = slice(first, first + step)
        u_cols = slice(hidden + first, hidden + first + step)
        d_cols = slice(2 * hidden + first, 2 * hidden + first + step)
        gate = dot(normed, w_ref[:, g_cols], ((1,), (0,)))
        upward = dot(normed, w_ref[:, u_cols], ((1,), (0,)))
        grad_hidden = dot(upstream, w_ref[:, d_cols], ((1,), (0,)))
        sigma = jax.nn.sigmoid(gate)
        active = gate * sigma
        hid = (active * upward).astype(BF)
        grad_gate = (grad_hidden * upward * sigma * (1.0 + gate * (1.0 - sigma))).astype(BF)
        grad_up = (grad_hidden * active).astype(BF)
        h_ref[:, g_cols] = hid
        d_ref[:, g_cols] = grad_gate
        d_ref[:, u_cols] = grad_up
        down = down + dot(hid, w_ref[:, d_cols], ((1,), (1,)))
        grad = grad + dot(grad_gate, w_ref[:, g_cols], ((1,), (1,)))
        grad = grad + dot(grad_up, w_ref[:, u_cols], ((1,), (1,)))
    down_ref[...] = down.astype(BF)
    dn_ref[...] = grad.astype(BF)


def result_kernel(*refs):
    *ins, select_ref, out_ref = refs
    for index in range(out_ref.shape[0]):
        r_ref, a_ref, b_ref = ins[3 * index : 3 * index + 3]
        total = r_ref[...] + (a_ref[...].astype(F32) + b_ref[...].astype(F32))
        out_ref[index] = dot(total.astype(BF), select_ref[...], ((1,), (1,))).astype(BF)


def resid_kernel(a_ref, b_ref, r_ref, dy_ref, gain_ref, w_ref, dr_ref, da_ref, dob_ref, term_ref):
    width = dob_ref.shape[1]
    grad = a_ref[...].astype(F32) + b_ref[...].astype(F32)
    scale_inv, unit = unit_norm(r_ref[...])
    total = dy_ref[...].astype(F32) + norm_backward(scale_inv, unit, gain_ref[1:2], grad)
    dr_ref[...] = total
    low = total.astype(BF)
    da_ref[...] = low
    dob_ref[...] = dot(low, w_ref[:, 3 * width : 4 * width], ((1,), (0,))).astype(BF)
    term = jnp.sum(unit * grad, axis=0, keepdims=True)
    term_ref[...] = jnp.broadcast_to(term, term_ref.shape)


def back_kernel(
    q_ref, k_ref, v_ref, dob_ref, lse_ref, keyseg_ref, queryseg_ref, cos_ref, sin_ref,
    dq_ref, far_ref, near_ref, own_ref,
):
    count, width = q_ref.shape
    visible = visible_of(keyseg_ref[...], queryseg_ref[...], count)
    cosine, sine = cos_ref[REACH * count :], sin_ref[REACH * count :]

    def pair(index, _):
        lanes = group(index)
        queries, keys, values = q_ref[:, lanes], k_ref[:, lanes], v_ref[:, lanes]
        upstream = dob_ref[:, lanes]
        dq = jnp.zeros((count, LANES), F32)
        dk = jnp.zeros(keys.shape, F32)
        dv = jnp.zeros(keys.shape, F32)
        for half in range(2):
            some_q, some_do = half_mask(queries, half), half_mask(upstream, half)
            scores = dot(keys, some_q, ((1,), (1,)))
            weight = jnp.exp(scores - lse_ref[pl.ds(2 * index + half, 1), :])
            probs = jnp.where(visible, weight, 0.0)
            grad_probs = dot(values, some_do, ((1,), (1,)))
            inner = jnp.sum(probs * grad_probs, axis=0, keepdims=True)
            grad_scores = (probs * (grad_probs - inner)).astype(BF)
            dk = dk + dot(grad_scores, some_q, ((1,), (0,)))
            dv = dv + dot(probs.astype(BF), some_do, ((1,), (0,)))
            dq = dq + dot(grad_scores, half_mask(keys, half), ((0,), (0,)))
        dq_ref[:, lanes] = unrope(dq * HEAD_DIM**-0.5, cosine, sine).astype(BF)
        for ref, first in ((far_ref, 0), (near_ref, count), (own_ref, 2 * count)):
            ref[:, lanes] = dk[first : first + count].astype(ref.dtype)
            ref[:, group(index + width // LANES)] = dv[first : first + count].astype(ref.dtype)
        return 0

    lax.fori_loop(0, width // LANES, pair, 0)


def mix_kernel(
    core_ref, dq_ref, own_ref, swap_ref, ret_ref, x_ref, w_ref, cos_ref, sin_ref,
    mix_ref, part_ref, term_ref,
):
    count, width = dq_ref.shape
    cosine, sine = cos_ref[REACH * count :], sin_ref[REACH * count :]
    swapped = swap_ref[...].astype(F32)
    total = own_ref[...] + jnp.where(core_ref[0, 0] == 0, swapped, 0.0) + ret_ref[...].astype(F32)
    mix_ref[:, :width] = dq_ref[...]
    for start in range(0, width, LANES):
        lanes = slice(start, start + LANES)
        into = slice(width + start, width + start + LANES)
        mix_ref[:, into] = unrope(total[:, lanes], cosine, sine).astype(BF)
    mix_ref[:, 2 * width :] = total[:, width:].astype(BF)
    part = dot(mix_ref[...], w_ref[:, : 3 * width], ((1,), (1,)))
    _, unit = unit_norm(x_ref[...].astype(F32))
    term = jnp.sum(unit * part, axis=0, keepdims=True)
    term_ref[...] = jnp.broadcast_to(term, term_ref.shape)
    part_ref[...] = part.astype(BF)


def grads_kernel(side, pairs, terms, *refs):
    *ins, out_ref = refs
    split = out_ref.shape[0]
    rows = slice(side * split, (side + 1) * split)
    column = 0
    place = 0
    for micro in pairs:
        wide = ins[place + 1].shape[1]
        for first in range(0, wide, GRAD_STEP):
            cols = slice(first, min(first + GRAD_STEP, wide))
            total = None
            for index in range(micro):
                left, right = ins[place + 2 * index], ins[place + 2 * index + 1]
                piece = dot(left[:, rows], right[:, cols], ((0,), (0,)))
                total = piece if total is None else total + piece
            out_ref[:, column + first : column + cols.stop] = total.astype(out_ref.dtype)
        column += wide
        place += 2 * micro
    if terms:
        one, two = None, None
        for index in range(terms):
            first, second = ins[place + 2 * index][0:1, rows], ins[place + 2 * index + 1][0:1, rows]
            one = first if one is None else one + first
            two = second if two is None else two + second
        line = lax.broadcasted_iota(jnp.int32, (LANES, split), 0)
        table = jnp.where(line == 0, one, jnp.where(line == 1, 0.5 * two, 0.0))
        out_ref[:, column : column + LANES] = table.T.astype(out_ref.dtype)


def weight_grads(side, kind, pairs, terms=()):
    split = pairs[0][0][0].shape[1] // 2
    args = [array for micro in pairs for pair in micro for array in pair]
    args += [array for pair in terms for array in pair]
    wide = sum(micro[0][1].shape[1] for micro in pairs) + (LANES if terms else 0)
    kernel = partial(grads_kernel, side, [len(micro) for micro in pairs], len(terms))
    return call(kernel, "weight_grads", [((split, wide), kind)], *args)[0]


def token_kernel(*refs):
    *ins, gain_ref, select_ref, out_ref = refs
    select = select_ref[...]
    for index in range(out_ref.shape[0]):
        a_ref, b_ref, x_ref, dr_ref = ins[4 * index : 4 * index + 4]
        grad = a_ref[...].astype(F32) + b_ref[...].astype(F32)
        scale_inv, unit = unit_norm(x_ref[...].astype(F32))
        rest = dr_ref[...] + norm_backward(scale_inv, unit, gain_ref[0:1], grad)
        total = jnp.zeros(rest.shape, F32)
        for _ in range(3):
            part = rest.astype(BF)
            rest = rest - part.astype(F32)
            total = total + dot(part, select, ((1,), (1,)))
        out_ref[index] = total


def body(
    inputs,
    cotangent,
    segments,
    qkv_weight,
    out_weight,
    gateup_weight,
    down_weight,
    norm_gains,
    qkv_momentum,
    out_momentum,
    gateup_momentum,
    down_momentum,
    gains_momentum,
    qkv_average,
    out_average,
    gateup_average,
    down_average,
    gains_average,
):
    masters = (qkv_weight, out_weight, gateup_weight, down_weight, norm_gains)
    micro, count, model = inputs.shape
    rows = qkv_weight.shape[0]
    width = qkv_weight.shape[2]
    hidden_units = down_weight.shape[1]
    span = (REACH + 1) * count
    devices = lax.axis_size("dp")
    rank = lax.axis_index("dp")
    core = rank % 2
    side = lax.axis_index("tensor")

    gain_columns = jnp.pad(norm_gains.astype(BF), ((0, 0), (0, 126)))
    first_group = jnp.concatenate(
        [
            qkv_weight.reshape(rows, 3 * width).astype(BF),
            out_weight.astype(BF),
            gain_columns,
        ],
        axis=1,
    )
    second_group = jnp.concatenate(
        [gateup_weight.reshape(rows, 2 * hidden_units).astype(BF), down_weight.astype(BF)],
        axis=1,
    )
    onward_chip = [(i, i + 2) for i in range(devices - 2)]
    fetched = lax.ppermute(
        lax.dynamic_index_in_dim(inputs, side, 0, keepdims=False), "dp", onward_chip
    )
    swapped = tensor_swap(fetched)
    two_back = jnp.stack(
        [jnp.where(side == 0, fetched, swapped), jnp.where(side == 0, swapped, fetched)]
    )
    one_back = core_swap(jnp.where(core == 0, inputs, two_back))

    order = feature_order(rows)[None, :]
    token_shape = ((micro, count, model), BF)
    select, x_own, dy_own = call(
        permute_kernel,
        "permute",
        [((model, model), BF), token_shape, token_shape],
        order,
        inputs,
        cotangent,
    )
    halo = call(halo_kernel, "halo", [((micro, 2 * count, model), BF)], two_back, one_back, select)[0]
    padded = jnp.concatenate([jnp.full((micro, REACH * count), -1, jnp.int32), segments], axis=1)
    start = rank * count
    key_segs = lax.dynamic_slice_in_dim(padded, start, span, 1)[:, :, None]
    query_segs = lax.dynamic_slice_in_dim(segments, start, count, 1)[:, None, :]
    cosine, sine = rope_tables(start - REACH * count, span)

    ring = RingGather(first_group)
    while ring.left > 1:
        ring.step()
    second_group = ring.step(second_group)
    whole_one = ring.finish()
    ring = RingGather(second_group)

    ahead = []
    for index in range(micro):
        normed, queries, keys, values, gains = call(
            qkv_kernel,
            "qkv",
            [
                ((count, model), BF),
                ((count, width), BF),
                ((span, width), BF),
                ((span, width), BF),
                ((8, model), F32),
            ],
            x_own[index],
            halo[index],
            whole_one,
            cosine,
            sine,
        )
        queries, keys, values = ring.step((queries, keys, values))
        attended, lse, branch = call(
            attend_kernel,
            "attend",
            [((count, width), BF), ((8, count), F32), ((count, model), BF)],
            queries,
            keys,
            values,
            key_segs[index],
            query_segs[index],
            whole_one,
        )
        branch = ring.step(branch)
        ahead.append((normed, queries, keys, values, attended, lse, branch, tensor_swap(branch)))
    whole_two = ring.finish()

    ffn = []
    for index in range(micro):
        branch, other = ahead[index][6:]
        resid, normed, hidden, grad_gateup, down, grad_normed = call(
            ffn_kernel,
            "ffn",
            [
                ((count, model), F32),
                ((count, model), BF),
                ((count, hidden_units), BF),
                ((count, 2 * hidden_units), BF),
                ((count, model), BF),
                ((count, model), BF),
            ],
            x_own[index],
            branch,
            other,
            dy_own[index],
            gains,
            whole_two,
        )
        ffn.append((resid, normed, hidden, grad_gateup, down, grad_normed, tensor_swap(grad_normed)))
    pairs = [
        [(f[1], f[3]) for f in ffn],
        [(dy_own[index], f[2]) for index, f in enumerate(ffn)],
    ]
    theirs = weight_grads(1, BF, pairs)
    mine = weight_grads(0, F32, pairs)
    reduce_two = RingScatter(mine, theirs, rows)

    core_flag = core.astype(jnp.int32).reshape(1, 1)
    behind = [(i + 2, i) for i in range(devices - 2)]
    back = []
    for index in range(micro):
        normed, queries, keys, values, attended, lse = ahead[index][:6]
        grad_resid, grad_branch, grad_attended, gain_term = call(
            resid_kernel,
            "resid",
            [
                ((count, model), F32),
                ((count, model), BF),
                ((count, width), BF),
                ((8, model), F32),
            ],
            ffn[index][5],
            ffn[index][6],
            ffn[index][0],
            dy_own[index],
            gains,
            whole_one,
        )
        grad_attended = reduce_two.step(grad_attended)
        grad_q, far, near, own = call(
            back_kernel,
            "back",
            [
                ((count, width), BF),
                ((count, 2 * width), F32),
                ((count, 2 * width), BF),
                ((count, 2 * width), F32),
            ],
            queries,
            keys,
            values,
            grad_attended,
            lse,
            key_segs[index],
            query_segs[index],
            cosine,
            sine,
        )
        far, near, own = reduce_two.step((far, near, own))
        from_core = core_swap(near)
        sent = far + jnp.where(core == 0, 0.0, from_core.astype(F32))
        returned = lax.ppermute(sent.astype(BF), "dp", behind)
        back.append((grad_resid, grad_branch, gain_term, grad_q, own, from_core, returned))
    mixed = []
    for index in range(micro):
        grad_q, own, from_core, returned = back[index][3:]
        returned = reduce_two.step(returned)
        grad_mixed, part, gain_term = call(
            mix_kernel,
            "mix",
            [((count, 3 * width), BF), ((count, model), BF), ((8, model), F32)],
            core_flag,
            grad_q,
            own,
            from_core,
            returned,
            x_own[index],
            whole_one,
            cosine,
            sine,
            smem=1,
        )
        mixed.append((grad_mixed, gain_term, part, tensor_swap(part)))
    pairs = [
        [(ahead[index][0], mixed[index][0]) for index in range(micro)],
        [(back[index][1], ahead[index][4]) for index in range(micro)],
    ]
    terms = [(mixed[index][1], back[index][2]) for index in range(micro)]
    theirs = weight_grads(1, BF, pairs, terms)
    mine = weight_grads(0, F32, pairs, terms)
    reduced_two = reduce_two.finish()
    reduce_one = RingScatter(mine, theirs, rows)

    args = []
    for f in ffn:
        args += [f[0], f[4], tensor_swap(f[4])]
    result = call(result_kernel, "result", [token_shape], *args, select)[0]
    args = []
    for index in range(micro):
        args += [mixed[index][2], mixed[index][3], x_own[index], back[index][0]]
    grad_tokens = call(
        token_kernel, "token", [((micro, count, model), F32)], *args, gains, select
    )[0]
    reduced_one = reduce_one.finish()
    gains_part = reduced_one[:, 4 * width : 4 * width + 2]
    totals = (
        reduced_one[:, : 3 * width].reshape(rows, 3, width),
        reduced_one[:, 3 * width : 4 * width],
        reduced_two[:, : 2 * hidden_units].reshape(rows, 2, hidden_units),
        reduced_two[:, 2 * hidden_units :],
        gains_part + tensor_swap(gains_part),
    )
    moments = (qkv_momentum, out_momentum, gateup_momentum, down_momentum, gains_momentum)
    averages = (qkv_average, out_average, gateup_average, down_average, gains_average)
    new_moments = tuple(
        (MOMENTUM * previous + gradient for previous, gradient in zip(moments, totals))
    )
    updated = tuple(
        (
            master - LEARN_RATE * (gradient + MOMENTUM * moment)
            for master, gradient, moment in zip(masters, totals, new_moments)
        )
    )
    averaged = tuple(
        (
            AVERAGE_RATE * previous + (1.0 - AVERAGE_RATE) * weight
            for previous, weight in zip(averages, updated)
        )
    )
    return (
        (result, grad_tokens)
        + tuple(totals)
        + new_moments
        + updated
        + averaged
    )


def solution(mesh):
    tokens = P(None, "dp", None)
    shards = (
        P("dp", None, "tensor"),
        P("dp", "tensor"),
        P("dp", None, "tensor"),
        P("dp", "tensor"),
        P("dp", None),
    )
    return jax.shard_map(
        body,
        mesh=mesh,
        in_specs=(tokens, tokens, P()) + shards * 3,
        out_specs=(tokens, tokens) + shards * 4,
        check_vma=False,
    )
```
